128 devices in a mesh: fsdp: 16 (over x, z), tp: 8 (over y, core).
Axes of the slice: x: 4, y: 4, z: 4, core: 2. Of those that a mesh axis runs over, the one named last changes fastest.
Arguments:
- weights: float32 [16384, 16384], P('fsdp', 'tp'), may hold values from -6 to 6
- owner: int32 [128], replicated, may hold values from 0 to 15, as said below
Outputs:
- rolled: bfloat16 [32768, 16384], P('fsdp', 'tp')
- rolled_scales: bfloat16 [256, 16384], P('fsdp', 'tp')
The draws below stay inside these ranges and needn't reach their ends.
Inputs may be any that keep to these rules, and one draw needn't show every extreme that they name: Trainer shard a holds blocks a * 8 to a * 8 + 7, as 8 runs of 1 block with one owner each and a different owner for each run; one rollout rank owns exactly 16 blocks.
All inputs are finite; a program needn't handle non-finite values.
Results may differ from the reference program's by a relative error of at most 0.0085.
Values may be sent and summed in bfloat16 or wider, within the bound.
No kernel may reach another device: no remote copies, remote signals or barrier semaphores. Data moves between devices by JAX's collectives and lax.ppermute only.
A program may use at most 320 MiB of HBM per device.

```python
import math
import jax
import jax.numpy as jnp
from jax import lax

K = 16384
BLOCK = 128
TILE = 128
COL_DEV = 2048
COLS = 16384
NB = 128
BPD = 8
PAIR = 1
UNITS = 8
CAP = 16
N_FSDP = 16
N_TP = 8


def draw_owner(key, part):
    busiest = jax.random.randint(jax.random.fold_in(key, 7), (), 0, N_FSDP).astype(jnp.int32)

    def per_sender(sender):
        sender_key = jax.random.fold_in(key, 100 + sender)
        order = jax.random.permutation(jax.random.fold_in(sender_key, 1), N_FSDP - 1).astype(jnp.int32)
        others = order + (order >= busiest).astype(jnp.int32)
        chosen = jnp.concatenate([busiest[None], others[:UNITS - 1]])
        shuffled = jax.random.permutation(jax.random.fold_in(sender_key, 2), chosen)
        return jnp.repeat(shuffled, PAIR)
    owners = jax.vmap(per_sender)(jnp.arange(N_FSDP, dtype=jnp.int32))
    return owners.reshape(NB).astype(jnp.int32)


def levels(rng, extent, pieces, low, high):
    def one(axis_at, shards_of):
        draws = jax.random.uniform(jax.random.fold_in(jax.random.fold_in(rng, 6), axis_at), (shards_of,), jnp.float32, low / len(pieces), high / len(pieces))
        return jnp.repeat(jnp.exp(draws), extent[axis_at] // shards_of).reshape((-1,) + (1,) * (len(extent) - axis_at - 1))

    loudness = one(*pieces[0])
    for cut in pieces[1:]:
        loudness = loudness * one(*cut)
    return loudness


def scatter_about(own_key, shape, spread, most, cuts=(), kind=jnp.bfloat16):
    drawn = spread * jax.random.normal(own_key, shape, jnp.float32)
    if cuts:
        drawn = drawn * levels(own_key, shape, cuts, -0.22, 0.18)
    return jnp.clip(drawn, -most, most).astype(kind)


def setup_inputs(seed: int = 0) -> dict:
    seeds = jax.random.split(jax.random.key(seed), 3)
    weights = scatter_about(seeds[0], (K, COLS), 1.0, 6.0, ((0, 16), (1, 8)), jnp.float32)
    owner = draw_owner(jax.random.fold_in(seeds[2], 71), 0)
    return dict(weights=weights, owner=owner)


def walsh_rows(matrix):
    length = matrix.shape[0]
    stride = 1
    while stride < length:
        grouped = matrix.reshape(length // (2 * stride), 2, stride, -1)
        upper_part = grouped[:, 0]
        lower_part = grouped[:, 1]
        matrix = jnp.stack([upper_part + lower_part, upper_part - lower_part], axis=1).reshape(length, -1)
        stride = stride * 2
    return matrix

def reference(weights, owner):
    blocks = jnp.arange(NB, dtype=jnp.int32)
    source = blocks // BPD
    earlier = (owner[:, None] == owner[None, :]) & (source[:, None] == source[None, :]) & (blocks[None, :] < blocks[:, None])
    rank_within = lax.optimization_barrier(jnp.sum(earlier.astype(jnp.int32), axis=1)).astype(jnp.int32)
    slots = ((owner * N_FSDP + source) * PAIR + rank_within).astype(jnp.int32)
    total_slots = N_FSDP * CAP

    def one_column_block(columns):
        rotated = walsh_rows(columns) * (1.0 / math.sqrt(K))
        grouped = rotated.reshape(NB, BLOCK, -1)
        largest = lax.optimization_barrier(jnp.max(jnp.abs(grouped), axis=1))
        block_scales = (largest + 1e-06).astype(jnp.bfloat16)
        quantized = (grouped / block_scales.astype(jnp.float32)[:, None, :]).astype(jnp.bfloat16)
        placed = jnp.zeros((total_slots, BLOCK, columns.shape[1]), jnp.bfloat16).at[slots].set(quantized)
        placed_scales = jnp.zeros((total_slots, columns.shape[1]), jnp.bfloat16).at[slots].set(block_scales)
        return (placed.reshape(total_slots * BLOCK, -1), placed_scales)
    stacked = weights.reshape(K, N_TP, COL_DEV).transpose(1, 0, 2)
    placed, placed_scales = lax.map(one_column_block, stacked)
    placed = placed.transpose(1, 0, 2).reshape(total_slots * BLOCK, COLS)
    placed_scales = placed_scales.transpose(1, 0, 2).reshape(total_slots, COLS)
    tiles = COLS // TILE

    def reorder(matrix):
        height = matrix.shape[0]
        return matrix.reshape(height, tiles // N_TP, N_TP, TILE).transpose(0, 2, 1, 3).reshape(height, COLS)
    return (reorder(placed), reorder(placed_scales))
```

```python
import functools

import jax
import jax.numpy as jnp
from jax import lax
from jax.experimental import pallas as pl
from jax.experimental.pallas import tpu as pltpu
from jax.sharding import PartitionSpec as P

BLOCK = 128
LANES = 128
GROUP = 16
EIGHT = 8
SHARDS = 16
F32 = jnp.float32
BF16 = jnp.bfloat16


def butterflies(values):
    values = list(values)
    span = 1
    while span < len(values):
        for base in range(0, len(values), 2 * span):
            for k in range(base, base + span):
                low, high = values[k], values[k + span]
                values[k], values[k + span] = low + high, low - high
        span *= 2
    return values


def swap_groups(arrays):
    arrays = list(arrays)
    group = lax.broadcasted_iota(jnp.int32, arrays[0].shape, 1) // GROUP
    for bit in (1, 2, 4):
        high_group = (group & bit) != 0
        shift = bit * GROUP
        for u in range(EIGHT):
            if u & bit:
                continue
            low, high = arrays[u], arrays[u | bit]
            arrays[u] = jnp.where(high_group, pltpu.roll(high, shift, 1), low)
            arrays[u | bit] = jnp.where(
                high_group, high, pltpu.roll(low, LANES - shift, 1)
            )
    return arrays


def swap_row_groups(value):
    row = lax.broadcasted_iota(jnp.int32, value.shape, 0)
    group = lax.broadcasted_iota(jnp.int32, value.shape, 1) // GROUP
    for bit in (1, 2, 4):
        row_bit = (row & bit) != 0
        group_bit = (group & bit) != 0
        shift = bit * GROUP
        up = pltpu.roll(pltpu.roll(value, EIGHT - bit, 0), shift, 1)
        down = pltpu.roll(pltpu.roll(value, bit, 0), LANES - shift, 1)
        value = jnp.where(row_bit == group_bit, value, jnp.where(row_bit, down, up))
    return value


def signs(size):
    both = lax.broadcasted_iota(jnp.int32, (size, size), 0) & lax.broadcasted_iota(
        jnp.int32, (size, size), 1
    )
    shift = size.bit_length() // 2
    while shift:
        both = both ^ (both >> shift)
        shift //= 2
    return (1 - 2 * (both & 1)).astype(F32).astype(BF16)


def local_kernel(w_ref, out_ref, sign_ref):
    @pl.when(pl.program_id(0) == 0)
    def _():
        sign_ref[...] = signs(256)

    rows = [
        jnp.dot(
            sign_ref[...],
            w_ref[pl.ds(256 * q, 256), :].astype(BF16),
            preferred_element_type=F32,
        )
        for q in range(4)
    ]
    rows = butterflies(rows)
    for tile in range(2):
        parts = [
            rows[j // 2][(j % 2) * BLOCK : (j % 2 + 1) * BLOCK, tile * LANES : (tile + 1) * LANES]
            * (1.0 / 32.0)
            for j in range(EIGHT)
        ]
        for g, part in enumerate(swap_groups(parts)):
            out_ref[0, g, tile] = part.astype(BF16)


def local_rotation(weights):
    rows, cols = weights.shape
    steps = cols // (2 * LANES)
    per_half = steps // 2
    return pl.pallas_call(
        local_kernel,
        grid=(steps,),
        in_specs=[pl.BlockSpec((rows, 2 * LANES), lambda s: (0, s))],
        out_specs=pl.BlockSpec(
            (1, EIGHT, 2, BLOCK, LANES),
            lambda s: (s // per_half, 0, s % per_half, 0, 0),
        ),
        out_shape=jax.ShapeDtypeStruct((2, EIGHT, EIGHT, BLOCK, LANES), BF16),
        scratch_shapes=[pltpu.VMEM((256, 256), BF16)],
        name="local_rotation",
    )(weights)


def quantize_kernel(owner_ref, in_ref, out_ref, held, scales, slots, slot_scales, sems):
    step = pl.program_id(0)

    @pl.when(step < EIGHT)
    def _():
        t = step
        for chunk in range(1):
            pass
        rotated = butterflies([in_ref[a, 0].astype(F32) for a in range(SHARDS)])
        for a in range(SHARDS):
            value = rotated[a] * 0.25
            largest = jnp.max(jnp.abs(value), axis=0, keepdims=True)
            scale = (largest + 1e-06).astype(BF16).astype(F32)
            scales[a, pl.ds(t, 1), :] = scale
            held[a, t] = (value * (1.0 / scale)).astype(BF16)

    @pl.when(step == 0)
    def _():
        slot_scales[...] = jnp.zeros_like(slot_scales)

    def send(a, buffer):
        return pltpu.make_async_copy(
            slots.at[buffer],
            out_ref.at[:, pl.ds(pl.multiple_of(a * BLOCK, BLOCK), BLOCK), :],
            sems.at[buffer],
        )

    @pl.when(step >= EIGHT)
    def _():
        a = step - EIGHT
        buffer = lax.rem(a, 2)

        @pl.when(a >= 2)
        def _():
            send(a - 2, buffer).wait()

        slots[buffer] = jnp.zeros(slots.shape[1:], BF16)
        blocks = swap_groups([held[a, t].astype(F32) for t in range(EIGHT)])
        block_scales = swap_row_groups(scales[a])
        for j in range(EIGHT):
            rank = owner_ref[a * EIGHT + j]
            slots[buffer, rank] = blocks[j].astype(BF16)
            slot_scales[rank, pl.ds(a, 1), :] = block_scales[j : j + 1]
        send(a, buffer).start()

    @pl.when(step == EIGHT + SHARDS - 1)
    def _():
        send(SHARDS - 2, 0).wait()
        send(SHARDS - 1, 1).wait()
        slots[0, :, pl.ds(0, SHARDS), :] = slot_scales[...].astype(BF16)
        last = pltpu.make_async_copy(
            slots.at[0, :, pl.ds(0, SHARDS), :],
            out_ref.at[:, pl.ds(SHARDS * BLOCK, SHARDS), :],
            sems.at[0],
        )
        last.start()
        last.wait()


def quantize_blocks(owner, received):
    out_rows = SHARDS * BLOCK + SHARDS
    return pl.pallas_call(
        quantize_kernel,
        grid_spec=pltpu.PrefetchScalarGridSpec(
            num_scalar_prefetch=1,
            grid=(EIGHT + SHARDS,),
            in_specs=[
                pl.BlockSpec(
                    (SHARDS, 1, BLOCK, LANES),
                    lambda s, _: (0, jnp.minimum(s, EIGHT - 1), 0, 0),
                )
            ],
            out_specs=pl.BlockSpec(memory_space=pl.ANY),
            scratch_shapes=[
                pltpu.VMEM((SHARDS, EIGHT, BLOCK, LANES), BF16),
                pltpu.VMEM((SHARDS, EIGHT, LANES), F32),
                pltpu.VMEM((2, SHARDS, BLOCK, LANES), BF16),
                pltpu.VMEM((SHARDS, SHARDS, LANES), F32),
                pltpu.SemaphoreType.DMA((2,)),
            ],
        ),
        out_shape=jax.ShapeDtypeStruct((SHARDS, out_rows, LANES), BF16),
        name="quantize_blocks",
    )(owner, received)


def place_kernel(in_ref, scale_in_ref, out_ref, scale_out_ref):
    for half in range(2):
        tiles = swap_groups([in_ref[half * EIGHT + g].astype(F32) for g in range(EIGHT)])
        for t in range(EIGHT):
            start = (2 * t + half) * LANES
            out_ref[:, start : start + LANES] = tiles[t].astype(BF16)

    @pl.when(pl.program_id(0) == 0)
    def _():
        for half in range(2):
            tiles = swap_groups(
                [scale_in_ref[half * EIGHT + g].astype(F32) for g in range(EIGHT)]
            )
            for t in range(EIGHT):
                start = (2 * t + half) * LANES
                scale_out_ref[:, start : start + LANES] = tiles[t].astype(BF16)


def place_columns(incoming):
    cols = SHARDS * LANES
    return pl.pallas_call(
        place_kernel,
        grid=(SHARDS,),
        in_specs=[
            pl.BlockSpec((SHARDS, BLOCK, LANES), lambda s: (0, s, 0)),
            pl.BlockSpec((SHARDS, SHARDS, LANES), lambda s: (0, BLOCK, 0)),
        ],
        out_specs=[
            pl.BlockSpec((BLOCK, cols), lambda s: (s, 0)),
            pl.BlockSpec((SHARDS, cols), lambda s: (0, 0)),
        ],
        out_shape=[
            jax.ShapeDtypeStruct((SHARDS * BLOCK, cols), BF16),
            jax.ShapeDtypeStruct((SHARDS, cols), BF16),
        ],
        name="place_columns",
    )(incoming, incoming)


def per_device(weights, owner):
    outgoing = local_rotation(weights).reshape(SHARDS * EIGHT, BLOCK, LANES)
    received = lax.all_to_all(outgoing, ("fsdp", "tp"), 0, 0, tiled=True)
    received = received.reshape(SHARDS, EIGHT, BLOCK, LANES)
    slotted = quantize_blocks(owner, received)
    incoming = lax.all_to_all(slotted, "fsdp", 0, 0, tiled=True)
    return tuple(place_columns(incoming))


def solution(mesh):
    return jax.shard_map(
        per_device,
        mesh=mesh,
        in_specs=(P("fsdp", "tp"), P()),
        out_specs=(P("fsdp", "tp"), P("fsdp", "tp")),
        check_vma=False,
    )
```

```python
import functools

import jax
import jax.numpy as jnp
from jax import lax
from jax.experimental import pallas as pl
from jax.experimental.pallas import tpu as pltpu
from jax.sharding import PartitionSpec as P

BLOCK = 128
LANES = 128
GROUP = 16
EIGHT = 8
SHARDS = 16
TILES = 4
PAIRS = 4
STEP_SLOTS = 4
F32 = jnp.float32
BF16 = jnp.bfloat16


def butterflies(values):
    values = list(values)
    span = 1
    while span < len(values):
        for base in range(0, len(values), 2 * span):
            for k in range(base, base + span):
                low, high = values[k], values[k + span]
                values[k], values[k + span] = low + high, low - high
        span *= 2
    return values


def parity_signs(bits, scale):
    shift = 4
    while shift:
        bits = bits ^ (bits >> shift)
        shift //= 2
    return jnp.where((bits & 1) == 0, scale, -scale).astype(BF16)


def identity(size):
    row = lax.broadcasted_iota(jnp.int32, (size, size), 0)
    col = lax.broadcasted_iota(jnp.int32, (size, size), 1)
    return jnp.where(row == col, 1.0, 0.0).astype(BF16)


def transposed(eye, value):
    return lax.dot_general(
        eye, value, (((1,), (1,)), ((), ())), preferred_element_type=F32
    ).astype(BF16)


def local_kernel(w_ref, out_ref, sign_ref, eye_ref):
    @pl.when(pl.program_id(0) == 0)
    def _():
        row = lax.broadcasted_iota(jnp.int32, (256, 256), 0)
        col = lax.broadcasted_iota(jnp.int32, (256, 256), 1)
        sign_ref[...] = parity_signs(row & col, 1.0 / 32.0)
        eye_ref[...] = identity(256)

    for pair in range(TILES // 2):
        lanes = slice(2 * pair * LANES, 2 * (pair + 1) * LANES)
        mixed = butterflies([w_ref[256 * q : 256 * (q + 1), lanes] for q in range(4)])
        for q in range(4):
            turned = transposed(eye_ref[...], mixed[q].astype(BF16))
            half = jnp.dot(turned, sign_ref[...], preferred_element_type=F32).astype(BF16)
            for tile in range(2):
                for g in range(EIGHT):
                    row = (tile * EIGHT + g) * GROUP
                    for side in range(2):
                        out_ref[0, g, 2 * pair + tile, 2 * q + side] = half[
                            row : row + GROUP, side * BLOCK : (side + 1) * BLOCK
                        ]


def local_rotation(weights):
    rows, cols = weights.shape
    steps = cols // (TILES * LANES)
    per_half = steps // 2
    return pl.pallas_call(
        local_kernel,
        grid=(steps,),
        in_specs=[pl.BlockSpec((rows, TILES * LANES), lambda s: (0, s))],
        out_specs=pl.BlockSpec(
            (1, EIGHT, TILES, EIGHT, GROUP, BLOCK),
            lambda s: (s // per_half, 0, s % per_half, 0, 0, 0),
        ),
        out_shape=jax.ShapeDtypeStruct((2, EIGHT, EIGHT, EIGHT, GROUP, BLOCK), BF16),
        scratch_shapes=[pltpu.VMEM((256, 256), BF16), pltpu.VMEM((256, 256), BF16)],
        name="local_rotation",
    )(weights)


def quantize_kernel(
    owner_ref, in_ref, out_ref,
    received, held, sign_ref, block_scales, slot_scales, tail,
    in_sems, out_sem, tail_sem,
):
    def fetch(pair):
        return pltpu.make_async_copy(
            in_ref.at[:, pl.ds(2 * pair, 2)], received.at[pair], in_sems.at[pair]
        )

    for pair in range(PAIRS):
        fetch(pair).start()

    slot_scales[...] = jnp.zeros_like(slot_scales)
    row = lax.broadcasted_iota(jnp.int32, (256, 256), 0)
    col = lax.broadcasted_iota(jnp.int32, (256, 256), 1)
    signs = parity_signs((row // GROUP) & (col // GROUP), 0.25)
    same = (row & (GROUP - 1)) == (col & (GROUP - 1))
    sign_ref[...] = jnp.where(same, signs.astype(F32), 0.0).astype(BF16)

    @pl.loop(0, PAIRS)
    def _(pair):
        fetch(pair).wait()
        lane = lax.broadcasted_iota(jnp.int32, (SHARDS * GROUP, LANES), 1)
        for t in range(EIGHT):
            stacked = jnp.concatenate(
                [
                    jnp.concatenate(
                        [received[pair, a * EIGHT + t, side] for a in range(SHARDS)], axis=0
                    )
                    for side in range(2)
                ],
                axis=1,
            )
            mixed = jnp.dot(sign_ref[...], stacked, preferred_element_type=F32)
            for side in range(2):
                value = mixed[:, side * BLOCK : (side + 1) * BLOCK]
                largest = jnp.max(jnp.abs(value), axis=1, keepdims=True)
                scale = (largest + 1e-06).astype(BF16).astype(F32)
                ratio = (value * (1.0 / scale)).astype(BF16)
                pltpu.store(
                    block_scales.at[side],
                    jnp.broadcast_to(scale, lane.shape),
                    mask=lane // GROUP == t,
                )
                for a in range(SHARDS):
                    held[2 * pair + side, a, t * GROUP : (t + 1) * GROUP, :] = ratio[
                        a * GROUP : (a + 1) * GROUP
                    ]
        slot_lane = lane[:GROUP] & (GROUP - 1)
        for side in range(2):
            for a in range(SHARDS):
                rank = owner_ref[a * EIGHT + 2 * pair + side]
                pltpu.make_async_copy(
                    held.at[2 * pair + side, a],
                    out_ref.at[rank, pl.ds(a * BLOCK, BLOCK)],
                    out_sem,
                ).start()
                pltpu.store(
                    slot_scales.at[rank],
                    block_scales[side, a * GROUP : (a + 1) * GROUP, :],
                    mask=slot_lane == a,
                )

    tail[...] = slot_scales[...].astype(BF16)
    tail_copy = pltpu.make_async_copy(
        tail, out_ref.at[:, pl.ds(SHARDS * BLOCK, GROUP), :], tail_sem
    )
    tail_copy.start()
    pltpu.make_async_copy(held, held, out_sem).wait()
    tail_copy.wait()


def quantize_blocks(owner, received):
    out_rows = SHARDS * BLOCK + GROUP
    sources = received.shape[0]
    return pl.pallas_call(
        quantize_kernel,
        in_specs=[
            pl.BlockSpec(memory_space=pltpu.SMEM),
            pl.BlockSpec(memory_space=pl.ANY),
        ],
        out_specs=pl.BlockSpec(memory_space=pl.ANY),
        scratch_shapes=[
            pltpu.VMEM((PAIRS, sources, 2, GROUP, BLOCK), BF16),
            pltpu.VMEM((EIGHT, SHARDS, BLOCK, BLOCK), BF16),
            pltpu.VMEM((256, 256), BF16),
            pltpu.VMEM((2, SHARDS * GROUP, LANES), F32),
            pltpu.VMEM((SHARDS, GROUP, LANES), F32),
            pltpu.VMEM((SHARDS, GROUP, LANES), BF16),
            pltpu.SemaphoreType.DMA((PAIRS,)),
            pltpu.SemaphoreType.DMA,
            pltpu.SemaphoreType.DMA,
        ],
        out_shape=jax.ShapeDtypeStruct((SHARDS, out_rows, LANES), BF16),
        name="quantize_blocks",
    )(owner, received)


def place_kernel(
    rank_ref, owner_ref, in_ref, scale_in_ref, out_ref, scale_out_ref, eye_ref
):
    @pl.when(pl.program_id(0) == 0)
    def _():
        eye_ref[...] = identity(BLOCK)
        stacked = jnp.concatenate([scale_in_ref[m] for m in range(SHARDS)], axis=0)
        by_column = transposed(eye_ref[...], stacked)
        for t in range(EIGHT):
            scale_out_ref[:, t * 2 * LANES : (t + 1) * 2 * LANES] = by_column[
                t * GROUP : (t + 1) * GROUP
            ]

    for slot in range(STEP_SLOTS):
        rows = slice(slot * BLOCK, (slot + 1) * BLOCK)
        first = (pl.program_id(0) * STEP_SLOTS + slot) * EIGHT
        taken = functools.reduce(
            jnp.logical_or, [owner_ref[first + j] == rank_ref[0] for j in range(EIGHT)]
        )

        @pl.when(taken)
        def _():
            for t in range(EIGHT):
                row = slot * BLOCK + t * GROUP
                stacked = jnp.concatenate(
                    [in_ref[m, row : row + GROUP, :] for m in range(SHARDS)], axis=0
                )
                out_ref[rows, t * 2 * LANES : (t + 1) * 2 * LANES] = transposed(
                    eye_ref[...], stacked
                )

        @pl.when(jnp.logical_not(taken))
        def _():
            out_ref[rows, :] = jnp.zeros((BLOCK, out_ref.shape[1]), BF16)


def place_columns(owner, incoming):
    cols = SHARDS * LANES
    step_rows = STEP_SLOTS * BLOCK
    rank = lax.axis_index("fsdp").astype(jnp.int32).reshape(1)
    return pl.pallas_call(
        place_kernel,
        grid=(SHARDS // STEP_SLOTS,),
        in_specs=[
            pl.BlockSpec(memory_space=pltpu.SMEM),
            pl.BlockSpec(memory_space=pltpu.SMEM),
            pl.BlockSpec((SHARDS, step_rows, LANES), lambda s: (0, s, 0)),
            pl.BlockSpec((SHARDS, SHARDS, LANES), lambda s: (0, BLOCK, 0)),
        ],
        out_specs=[
            pl.BlockSpec((step_rows, cols), lambda s: (s, 0)),
            pl.BlockSpec((SHARDS, cols), lambda s: (0, 0)),
        ],
        out_shape=[
            jax.ShapeDtypeStruct((SHARDS * BLOCK, cols), BF16),
            jax.ShapeDtypeStruct((SHARDS, cols), BF16),
        ],
        scratch_shapes=[pltpu.VMEM((BLOCK, BLOCK), BF16)],
        name="place_columns",
    )(rank, owner, incoming, incoming)


def per_device(weights, owner):
    outgoing = local_rotation(weights).reshape(SHARDS * EIGHT, EIGHT * GROUP, BLOCK)
    received = lax.all_to_all(outgoing, ("fsdp", "tp"), 0, 0, tiled=True)
    received = received.reshape(SHARDS * EIGHT, EIGHT, GROUP, BLOCK)
    slotted = quantize_blocks(owner, received)
    incoming = lax.all_to_all(slotted, "fsdp", 0, 0, tiled=True)
    return tuple(place_columns(owner, incoming))


def solution(mesh):
    return jax.shard_map(
        per_device,
        mesh=mesh,
        in_specs=(P("fsdp", "tp"), P()),
        out_specs=(P("fsdp", "tp"), P("fsdp", "tp")),
        check_vma=False,
    )
```

```python
import functools

import jax
import jax.numpy as jnp
from jax import lax
from jax.experimental import pallas as pl
from jax.experimental.pallas import tpu as pltpu
from jax.sharding import PartitionSpec as P

BLOCK = 128
LANES = 128
GROUP = 16
EIGHT = 8
SHARDS = 16
TILES = 4
PAIRS = 4
STEP_SLOTS = 4
F32 = jnp.float32
BF16 = jnp.bfloat16


def butterflies(values):
    values = list(values)
    span = 1
    while span < len(values):
        for base in range(0, len(values), 2 * span):
            for k in range(base, base + span):
                low, high = values[k], values[k + span]
                values[k], values[k + span] = low + high, low - high
        span *= 2
    return values


def parity_signs(bits, scale):
    shift = 4
    while shift:
        bits = bits ^ (bits >> shift)
        shift //= 2
    return jnp.where((bits & 1) == 0, scale, -scale).astype(BF16)


def identity(size):
    row = lax.broadcasted_iota(jnp.int32, (size, size), 0)
    col = lax.broadcasted_iota(jnp.int32, (size, size), 1)
    return jnp.where(row == col, 1.0, 0.0).astype(BF16)


def transposed(eye, value):
    return lax.dot_general(
        eye, value, (((1,), (1,)), ((), ())), preferred_element_type=F32
    ).astype(BF16)


def local_kernel(w_ref, out_ref, sign_ref, eye_ref):
    @pl.when(pl.program_id(0) == 0)
    def _():
        row = lax.broadcasted_iota(jnp.int32, (256, 256), 0)
        col = lax.broadcasted_iota(jnp.int32, (256, 256), 1)
        sign_ref[...] = parity_signs(row & col, 1.0 / 32.0)
        eye_ref[...] = identity(256)

    for pair in range(TILES // 2):
        lanes = slice(2 * pair * LANES, 2 * (pair + 1) * LANES)
        mixed = butterflies([w_ref[256 * q : 256 * (q + 1), lanes] for q in range(4)])
        for q in range(4):
            turned = transposed(eye_ref[...], mixed[q].astype(BF16))
            half = jnp.dot(turned, sign_ref[...], preferred_element_type=F32).astype(BF16)
            for tile in range(2):
                for g in range(EIGHT):
                    row = (tile * EIGHT + g) * GROUP
                    for side in range(2):
                        out_ref[0, g, 2 * pair + tile, 2 * q + side] = half[
                            row : row + GROUP, side * BLOCK : (side + 1) * BLOCK
                        ]


def local_rotation(weights):
    rows, cols = weights.shape
    steps = cols // (TILES * LANES)
    per_half = steps // 2
    return pl.pallas_call(
        local_kernel,
        grid=(steps,),
        in_specs=[pl.BlockSpec((rows, TILES * LANES), lambda s: (0, s))],
        out_specs=pl.BlockSpec(
            (1, EIGHT, TILES, EIGHT, GROUP, BLOCK),
            lambda s: (s // per_half, 0, s % per_half, 0, 0, 0),
        ),
        out_shape=jax.ShapeDtypeStruct((2, EIGHT, EIGHT, EIGHT, GROUP, BLOCK), BF16),
        scratch_shapes=[pltpu.VMEM((256, 256), BF16), pltpu.VMEM((256, 256), BF16)],
        name="local_rotation",
    )(weights)


def quantize_kernel(
    owner_ref, in_ref, out_ref,
    received, held, sign_ref, block_scales, slot_scales, tail,
    in_sems, out_sem, tail_sem,
):
    def fetch(pair):
        return pltpu.make_async_copy(
            in_ref.at[:, pl.ds(2 * pair, 2)], received.at[pair], in_sems.at[pair]
        )

    for pair in range(PAIRS):
        fetch(pair).start()

    slot_scales[...] = jnp.zeros_like(slot_scales)
    row = lax.broadcasted_iota(jnp.int32, (256, 256), 0)
    col = lax.broadcasted_iota(jnp.int32, (256, 256), 1)
    signs = parity_signs((row // GROUP) & (col // GROUP), 0.25)
    same = (row & (GROUP - 1)) == (col & (GROUP - 1))
    sign_ref[...] = jnp.where(same, signs.astype(F32), 0.0).astype(BF16)

    @pl.loop(0, PAIRS)
    def _(pair):
        fetch(pair).wait()
        lane = lax.broadcasted_iota(jnp.int32, (SHARDS * GROUP, LANES), 1)
        for t in range(EIGHT):
            stacked = jnp.concatenate(
                [
                    jnp.concatenate(
                        [received[pair, a * EIGHT + t, side] for a in range(SHARDS)], axis=0
                    )
                    for side in range(2)
                ],
                axis=1,
            )
            mixed = jnp.dot(sign_ref[...], stacked, preferred_element_type=F32)
            for side in range(2):
                value = mixed[:, side * BLOCK : (side + 1) * BLOCK]
                largest = jnp.max(jnp.abs(value), axis=1, keepdims=True)
                scale = (largest + 1e-06).astype(BF16).astype(F32)
                ratio = (value * (1.0 / scale)).astype(BF16)
                pltpu.store(
                    block_scales.at[side],
                    jnp.broadcast_to(scale, lane.shape),
                    mask=lane // GROUP == t,
                )
                for a in range(SHARDS):
                    held[2 * pair + side, a, t * GROUP : (t + 1) * GROUP, :] = ratio[
                        a * GROUP : (a + 1) * GROUP
                    ]
        slot_lane = lane[:GROUP] & (GROUP - 1)
        for side in range(2):
            for a in range(SHARDS):
                rank = owner_ref[a * EIGHT + 2 * pair + side]
                pltpu.make_async_copy(
                    held.at[2 * pair + side, a],
                    out_ref.at[rank, pl.ds(a * BLOCK, BLOCK)],
                    out_sem,
                ).start()
                pltpu.store(
                    slot_scales.at[rank],
                    block_scales[side, a * GROUP : (a + 1) * GROUP, :],
                    mask=slot_lane == a,
                )

    tail[...] = slot_scales[...].astype(BF16)
    tail_copy = pltpu.make_async_copy(
        tail, out_ref.at[:, pl.ds(SHARDS * BLOCK, GROUP), :], tail_sem
    )
    tail_copy.start()
    pltpu.make_async_copy(held, held, out_sem).wait()
    tail_copy.wait()


def quantize_blocks(owner, received):
    out_rows = SHARDS * BLOCK + GROUP
    sources = received.shape[0]
    return pl.pallas_call(
        quantize_kernel,
        in_specs=[
            pl.BlockSpec(memory_space=pltpu.SMEM),
            pl.BlockSpec(memory_space=pl.ANY),
        ],
        out_specs=pl.BlockSpec(memory_space=pl.ANY),
        scratch_shapes=[
            pltpu.VMEM((PAIRS, sources, 2, GROUP, BLOCK), BF16),
            pltpu.VMEM((EIGHT, SHARDS, BLOCK, BLOCK), BF16),
            pltpu.VMEM((256, 256), BF16),
            pltpu.VMEM((2, SHARDS * GROUP, LANES), F32),
            pltpu.VMEM((SHARDS, GROUP, LANES), F32),
            pltpu.VMEM((SHARDS, GROUP, LANES), BF16),
            pltpu.SemaphoreType.DMA((PAIRS,)),
            pltpu.SemaphoreType.DMA,
            pltpu.SemaphoreType.DMA,
        ],
        out_shape=jax.ShapeDtypeStruct((SHARDS, out_rows, LANES), BF16),
        name="quantize_blocks",
    )(owner, received)


def place_kernel(
    owner_ref, in_ref, scale_in_ref, out_ref, scale_out_ref, eye_ref
):
    @pl.when(pl.program_id(0) == 0)
    def _():
        eye_ref[...] = identity(BLOCK)
        stacked = jnp.concatenate([scale_in_ref[m] for m in range(SHARDS)], axis=0)
        by_column = transposed(eye_ref[...], stacked)
        for t in range(EIGHT):
            scale_out_ref[:, t * 2 * LANES : (t + 1) * 2 * LANES] = by_column[
                t * GROUP : (t + 1) * GROUP
            ]

    rank = lax.axis_index("fsdp")
    for slot in range(STEP_SLOTS):
        rows = slice(slot * BLOCK, (slot + 1) * BLOCK)
        first = (pl.program_id(0) * STEP_SLOTS + slot) * EIGHT
        taken = functools.reduce(
            jnp.logical_or, [owner_ref[first + j] == rank for j in range(EIGHT)]
        )

        @pl.when(taken)
        def _():
            for t in range(EIGHT):
                row = slot * BLOCK + t * GROUP
                stacked = jnp.concatenate(
                    [in_ref[m, row : row + GROUP, :] for m in range(SHARDS)], axis=0
                )
                out_ref[rows, t * 2 * LANES : (t + 1) * 2 * LANES] = transposed(
                    eye_ref[...], stacked
                )

        @pl.when(jnp.logical_not(taken))
        def _():
            out_ref[rows, :] = jnp.zeros((BLOCK, out_ref.shape[1]), BF16)


def place_columns(owner, incoming):
    cols = SHARDS * LANES
    step_rows = STEP_SLOTS * BLOCK
    return pl.pallas_call(
        place_kernel,
        grid=(SHARDS // STEP_SLOTS,),
        in_specs=[
            pl.BlockSpec(memory_space=pltpu.SMEM),
            pl.BlockSpec((SHARDS, step_rows, LANES), lambda s: (0, s, 0)),
            pl.BlockSpec((SHARDS, SHARDS, LANES), lambda s: (0, BLOCK, 0)),
        ],
        out_specs=[
            pl.BlockSpec((step_rows, cols), lambda s: (s, 0)),
            pl.BlockSpec((SHARDS, cols), lambda s: (0, 0)),
        ],
        out_shape=[
            jax.ShapeDtypeStruct((SHARDS * BLOCK, cols), BF16),
            jax.ShapeDtypeStruct((SHARDS, cols), BF16),
        ],
        scratch_shapes=[pltpu.VMEM((BLOCK, BLOCK), BF16)],
        name="place_columns",
    )(owner, incoming, incoming)


def per_device(weights, owner):
    outgoing = local_rotation(weights).reshape(SHARDS * EIGHT, EIGHT * GROUP, BLOCK)
    received = lax.all_to_all(outgoing, ("fsdp", "tp"), 0, 0, tiled=True)
    received = received.reshape(SHARDS * EIGHT, EIGHT, GROUP, BLOCK)
    slotted = quantize_blocks(owner, received)
    incoming = lax.all_to_all(slotted, "fsdp", 0, 0, tiled=True)
    return tuple(place_columns(owner, incoming))


def solution(mesh):
    return jax.shard_map(
        per_device,
        mesh=mesh,
        in_specs=(P("fsdp", "tp"), P()),
        out_specs=(P("fsdp", "tp"), P("fsdp", "tp")),
        check_vma=False,
    )
```

```python
import functools

import jax
import jax.numpy as jnp
from jax import lax
from jax.experimental import pallas as pl
from jax.experimental.pallas import tpu as pltpu
from jax.sharding import PartitionSpec as P

BLOCK = 128
LANES = 128
GROUP = 16
EIGHT = 8
SHARDS = 16
TILES = 4
PAIRS = 4
STEP_SLOTS = 4
SIDE = 4
PACKED = 12
META_RANK, META_POS, META_SLOT, META_HOT, META_FITS, META_OWNER = range(6)
F32 = jnp.float32
BF16 = jnp.bfloat16


def butterflies(values):
    values = list(values)
    span = 1
    while span < len(values):
        for base in range(0, len(values), 2 * span):
            for k in range(base, base + span):
                low, high = values[k], values[k + span]
                values[k], values[k + span] = low + high, low - high
        span *= 2
    return values


def parity_signs(bits, scale):
    shift = 4
    while shift:
        bits = bits ^ (bits >> shift)
        shift //= 2
    return jnp.where((bits & 1) == 0, scale, -scale).astype(BF16)


def identity(size):
    row = lax.broadcasted_iota(jnp.int32, (size, size), 0)
    col = lax.broadcasted_iota(jnp.int32, (size, size), 1)
    return jnp.where(row == col, 1.0, 0.0).astype(BF16)


def transposed(eye, value):
    return lax.dot_general(
        eye, value, (((1,), (1,)), ((), ())), preferred_element_type=F32
    ).astype(BF16)


def fill_tables(owner_row, me, meta_ref):
    shape = (BLOCK, BLOCK)
    by_lane = jnp.broadcast_to(owner_row.astype(F32), shape)
    by_row = by_lane.T
    row = lax.broadcasted_iota(jnp.int32, shape, 0)
    lane = lax.broadcasted_iota(jnp.int32, shape, 1)
    equal = by_lane == by_row

    def count(mask, axis):
        total = jnp.sum(jnp.where(mask, 1.0, 0.0), axis=axis, keepdims=True)
        return total.astype(jnp.int32)

    total = count(equal, 0)
    position = count(equal & (row < lane), 0)
    position_by_row = count(equal & (lane < row), 1)
    hot = jnp.max(jnp.where(total == SHARDS, owner_row, -1), axis=1, keepdims=True)
    x, z = hot >> 2, hot & (SIDE - 1)
    around = [
        (((x + 1) & (SIDE - 1)) << 2) | z,
        (((x - 1) & (SIDE - 1)) << 2) | z,
        (x << 2) | ((z + 1) & (SIDE - 1)),
        (x << 2) | ((z - 1) & (SIDE - 1)),
    ]
    is_hot = owner_row == hot
    is_near = functools.reduce(jnp.logical_or, [owner_row == near for near in around])
    load = jnp.where(is_hot, 0, total + is_near.astype(jnp.int32))
    fits = (jnp.max(load, axis=1, keepdims=True) <= PACKED) & (hot >= 0)
    fits = jnp.broadcast_to(fits.astype(jnp.int32), owner_row.shape) != 0
    over = is_hot & (position >= PACKED) & fits
    rank = owner_row
    for d, near in enumerate(around):
        rank = jnp.where(over & (position == PACKED + d), near, rank)
    block = lane[:1]
    position = jnp.where(fits, jnp.where(over, PACKED - 1, position), block >> 3)
    mine = (by_row == me.astype(F32)) & ((row >> 3) == lane)
    slot = jnp.sum(
        jnp.where(mine, (position_by_row + 1).astype(F32), 0.0), axis=0, keepdims=True
    ).astype(jnp.int32) - 1
    slot = jnp.where(fits | (slot < 0), slot, block)
    meta_ref[META_RANK : META_RANK + 1, :] = rank
    meta_ref[META_POS : META_POS + 1, :] = position
    meta_ref[META_SLOT : META_SLOT + 1, :] = slot
    meta_ref[META_HOT : META_HOT + 1, :] = jnp.broadcast_to(hot, owner_row.shape)
    meta_ref[META_FITS : META_FITS + 1, :] = fits.astype(jnp.int32)
    meta_ref[META_OWNER : META_OWNER + 1, :] = owner_row


def local_kernel(owner_ref, w_ref, out_ref, meta_ref, sign_ref, eye_ref):
    @pl.when(pl.program_id(0) == 0)
    def _():
        row = lax.broadcasted_iota(jnp.int32, (256, 256), 0)
        col = lax.broadcasted_iota(jnp.int32, (256, 256), 1)
        sign_ref[...] = parity_signs(row & col, 1.0 / 32.0)
        eye_ref[...] = identity(256)
        fill_tables(owner_ref[...], lax.axis_index("fsdp"), meta_ref)

    for pair in range(TILES // 2):
        lanes = slice(2 * pair * LANES, 2 * (pair + 1) * LANES)
        mixed = butterflies([w_ref[256 * q : 256 * (q + 1), lanes] for q in range(4)])
        for q in range(4):
            turned = transposed(eye_ref[...], mixed[q].astype(BF16))
            half = jnp.dot(turned, sign_ref[...], preferred_element_type=F32).astype(BF16)
            for tile in range(2):
                for g in range(EIGHT):
                    row = (tile * EIGHT + g) * GROUP
                    for side in range(2):
                        out_ref[0, g, 2 * pair + tile, 2 * q + side] = half[
                            row : row + GROUP, side * BLOCK : (side + 1) * BLOCK
                        ]


def local_rotation(owner, weights):
    rows, cols = weights.shape
    steps = cols // (TILES * LANES)
    per_half = steps // 2
    return pl.pallas_call(
        local_kernel,
        grid=(steps,),
        in_specs=[
            pl.BlockSpec((1, BLOCK), lambda s: (0, 0)),
            pl.BlockSpec((rows, TILES * LANES), lambda s: (0, s)),
        ],
        out_specs=[
            pl.BlockSpec(
                (1, EIGHT, TILES, EIGHT, GROUP, BLOCK),
                lambda s: (s // per_half, 0, s % per_half, 0, 0, 0),
            ),
            pl.BlockSpec((EIGHT, BLOCK), lambda s: (0, 0)),
        ],
        out_shape=[
            jax.ShapeDtypeStruct((2, EIGHT, EIGHT, EIGHT, GROUP, BLOCK), BF16),
            jax.ShapeDtypeStruct((EIGHT, BLOCK), jnp.int32),
        ],
        scratch_shapes=[pltpu.VMEM((256, 256), BF16), pltpu.VMEM((256, 256), BF16)],
        name="local_rotation",
    )(owner.reshape(1, BLOCK), weights)


def quantize_kernel(
    meta_ref, in_ref, out_ref,
    received, held, sign_ref, block_scales, slot_scales, tail,
    in_sems, out_sem, tail_sem,
):
    def fetch(pair):
        return pltpu.make_async_copy(
            in_ref.at[:, pl.ds(2 * pair, 2)], received.at[pair], in_sems.at[pair]
        )

    for pair in range(PAIRS):
        fetch(pair).start()

    slot_scales[...] = jnp.zeros_like(slot_scales)
    row = lax.broadcasted_iota(jnp.int32, (256, 256), 0)
    col = lax.broadcasted_iota(jnp.int32, (256, 256), 1)
    signs = parity_signs((row // GROUP) & (col // GROUP), 0.25)
    same = (row & (GROUP - 1)) == (col & (GROUP - 1))
    sign_ref[...] = jnp.where(same, signs.astype(F32), 0.0).astype(BF16)

    @pl.loop(0, PAIRS)
    def _(pair):
        fetch(pair).wait()
        lane = lax.broadcasted_iota(jnp.int32, (SHARDS * GROUP, LANES), 1)
        for t in range(EIGHT):
            stacked = jnp.concatenate(
                [
                    jnp.concatenate(
                        [received[pair, a * EIGHT + t, side] for a in range(SHARDS)], axis=0
                    )
                    for side in range(2)
                ],
                axis=1,
            )
            mixed = jnp.dot(sign_ref[...], stacked, preferred_element_type=F32)
            for side in range(2):
                value = mixed[:, side * BLOCK : (side + 1) * BLOCK]
                largest = jnp.max(jnp.abs(value), axis=1, keepdims=True)
                scale = (largest + 1e-06).astype(BF16).astype(F32)
                ratio = (value * (1.0 / scale)).astype(BF16)
                pltpu.store(
                    block_scales.at[side],
                    jnp.broadcast_to(scale, lane.shape),
                    mask=lane // GROUP == t,
                )
                for a in range(SHARDS):
                    held[2 * pair + side, a, t * GROUP : (t + 1) * GROUP, :] = ratio[
                        a * GROUP : (a + 1) * GROUP
                    ]
        slot_lane = lane[:GROUP] & (GROUP - 1)
        for side in range(2):
            for a in range(SHARDS):
                block = a * EIGHT + 2 * pair + side
                start = pl.multiple_of(meta_ref[META_POS, block] * BLOCK, BLOCK)
                pltpu.make_async_copy(
                    held.at[2 * pair + side, a],
                    out_ref.at[meta_ref[META_RANK, block], pl.ds(start, BLOCK)],
                    out_sem,
                ).start()
                pltpu.store(
                    slot_scales.at[meta_ref[META_OWNER, block]],
                    block_scales[side, a * GROUP : (a + 1) * GROUP, :],
                    mask=slot_lane == a,
                )

    tail[...] = slot_scales[...].astype(BF16)
    tail_copy = pltpu.make_async_copy(
        tail, out_ref.at[:, pl.ds(out_ref.shape[1] - GROUP, GROUP), :], tail_sem
    )
    tail_copy.start()
    pltpu.make_async_copy(held, held, out_sem).wait()
    tail_copy.wait()


def quantize_blocks(meta, received, capacity):
    out_rows = capacity * BLOCK + GROUP
    sources = received.shape[0]
    return pl.pallas_call(
        quantize_kernel,
        in_specs=[
            pl.BlockSpec(memory_space=pltpu.SMEM),
            pl.BlockSpec(memory_space=pl.ANY),
        ],
        out_specs=pl.BlockSpec(memory_space=pl.ANY),
        scratch_shapes=[
            pltpu.VMEM((PAIRS, sources, 2, GROUP, BLOCK), BF16),
            pltpu.VMEM((EIGHT, SHARDS, BLOCK, BLOCK), BF16),
            pltpu.VMEM((256, 256), BF16),
            pltpu.VMEM((2, SHARDS * GROUP, LANES), F32),
            pltpu.VMEM((SHARDS, GROUP, LANES), F32),
            pltpu.VMEM((SHARDS, GROUP, LANES), BF16),
            pltpu.SemaphoreType.DMA((PAIRS,)),
            pltpu.SemaphoreType.DMA,
            pltpu.SemaphoreType.DMA,
        ],
        out_shape=jax.ShapeDtypeStruct((SHARDS, out_rows, LANES), BF16),
        name="quantize_blocks",
    )(meta, received)


def place_block(eye, source, target):
    for t in range(EIGHT):
        stacked = jnp.concatenate(
            [source[m, t * GROUP : (t + 1) * GROUP, :] for m in range(SHARDS)], axis=0
        )
        target[:, t * 2 * LANES : (t + 1) * 2 * LANES] = transposed(eye, stacked)


def place_kernel(capacity, meta_ref, *refs):
    ins, (scale_in_ref, out_ref, scale_out_ref, eye_ref) = refs[:STEP_SLOTS], refs[STEP_SLOTS:]

    @pl.when(pl.program_id(0) == 0)
    def _():
        eye_ref[...] = identity(BLOCK)
        stacked = jnp.concatenate([scale_in_ref[m] for m in range(SHARDS)], axis=0)
        by_column = transposed(eye_ref[...], stacked)
        for t in range(EIGHT):
            scale_out_ref[:, t * 2 * LANES : (t + 1) * 2 * LANES] = by_column[
                t * GROUP : (t + 1) * GROUP
            ]

    for k in range(STEP_SLOTS):
        target = out_ref.at[pl.ds(k * BLOCK, BLOCK), :]
        source = meta_ref[META_SLOT, pl.program_id(0) * STEP_SLOTS + k]
        taken = (source >= 0) & (source < capacity)

        @pl.when(taken)
        def _():
            place_block(eye_ref[...], ins[k], target)

        @pl.when(jnp.logical_not(taken))
        def _():
            target[...] = jnp.zeros(target.shape, BF16)


def place_columns(meta, incoming, capacity):
    cols = SHARDS * LANES
    step_rows = STEP_SLOTS * BLOCK

    def slot_map(k):
        def index(s, meta_ref):
            source = meta_ref[META_SLOT, s * STEP_SLOTS + k]
            return (0, jnp.clip(source, 0, capacity - 1), 0)

        return index

    return pl.pallas_call(
        functools.partial(place_kernel, capacity),
        grid_spec=pltpu.PrefetchScalarGridSpec(
            num_scalar_prefetch=1,
            grid=(SHARDS // STEP_SLOTS,),
            in_specs=[
                pl.BlockSpec((SHARDS, BLOCK, LANES), slot_map(k)) for k in range(STEP_SLOTS)
            ]
            + [pl.BlockSpec((SHARDS, GROUP, LANES), lambda s, _: (0, capacity * EIGHT, 0))],
            out_specs=[
                pl.BlockSpec((step_rows, cols), lambda s, _: (s, 0)),
                pl.BlockSpec((SHARDS, cols), lambda s, _: (0, 0)),
            ],
            scratch_shapes=[pltpu.VMEM((BLOCK, BLOCK), BF16)],
        ),
        out_shape=[
            jax.ShapeDtypeStruct((SHARDS * BLOCK, cols), BF16),
            jax.ShapeDtypeStruct((SHARDS, cols), BF16),
        ],
        cost_estimate=pl.CostEstimate(
            flops=2 * SHARDS * BLOCK * BLOCK * cols,
            bytes_accessed=4 * SHARDS * BLOCK * cols,
            transcendentals=0,
        ),
        name="place_columns",
    )(meta, *[incoming] * (STEP_SLOTS + 1))


def copy_kernel(in_ref, out_ref):
    out_ref[...] = in_ref[...]


def last_position(incoming):
    shape = (SHARDS, BLOCK, LANES)
    return pl.pallas_call(
        copy_kernel,
        grid=(1,),
        in_specs=[pl.BlockSpec(shape, lambda s: (0, PACKED - 1, 0))],
        out_specs=pl.BlockSpec(shape, lambda s: (0, 0, 0)),
        out_shape=jax.ShapeDtypeStruct(shape, BF16),
        name="last_position",
    )(incoming)


def patch_kernel(
    meta_ref, near_0, near_1, near_2, near_3, _, out_ref, nears, buffers, eye_ref, in_sem, sem
):
    @pl.when(meta_ref[META_HOT, 0] == lax.axis_index("fsdp"))
    def _():
        loads = [
            pltpu.make_async_copy(near, nears.at[d], in_sem.at[d])
            for d, near in enumerate((near_0, near_1, near_2, near_3))
        ]
        for load in loads:
            load.start()
        eye_ref[...] = identity(BLOCK)
        stores = []
        for d, load in enumerate(loads):
            load.wait()
            place_block(eye_ref[...], nears.at[d], buffers.at[d])
            stores.append(
                pltpu.make_async_copy(
                    buffers.at[d], out_ref.at[pl.ds((PACKED + d) * BLOCK, BLOCK), :], sem.at[d]
                )
            )
            stores[-1].start()
        for store in stores:
            store.wait()


def patch_hot_rank(meta, rolled, nears):
    cols = rolled.shape[1]
    return pl.pallas_call(
        patch_kernel,
        in_specs=[pl.BlockSpec(memory_space=pltpu.SMEM)]
        + [pl.BlockSpec(memory_space=pl.ANY)] * 5,
        out_specs=pl.BlockSpec(memory_space=pl.ANY),
        out_shape=jax.ShapeDtypeStruct(rolled.shape, rolled.dtype),
        scratch_shapes=[
            pltpu.VMEM((4, SHARDS, BLOCK, LANES), BF16),
            pltpu.VMEM((4, BLOCK, cols), BF16),
            pltpu.VMEM((BLOCK, BLOCK), BF16),
            pltpu.SemaphoreType.DMA((4,)),
            pltpu.SemaphoreType.DMA((4,)),
        ],
        input_output_aliases={5: 0},
        name="patch_hot_rank",
    )(meta, *nears, rolled)


def shifted(value, dx, dz):
    pairs = []
    for source in range(SHARDS):
        x, z = divmod(source, SIDE)
        pairs.append((source, (x + dx) % SIDE * SIDE + (z + dz) % SIDE))
    return lax.ppermute(value, "fsdp", pairs)


def general(meta, received):
    slotted = quantize_blocks(meta, received, SHARDS)
    incoming = lax.all_to_all(slotted, "fsdp", 0, 0, tiled=True)
    return tuple(place_columns(meta, incoming, SHARDS))


def packed(meta, received):
    slotted = quantize_blocks(meta, received, PACKED)
    incoming = lax.all_to_all(slotted, "fsdp", 0, 0, tiled=True)
    foreign = last_position(incoming)
    nears = [shifted(foreign, dx, dz) for dx, dz in ((-1, 0), (1, 0), (0, -1), (0, 1))]
    rolled, rolled_scales = place_columns(meta, incoming, PACKED)
    return patch_hot_rank(meta, rolled, nears), rolled_scales


def per_device(weights, owner):
    outgoing, meta = local_rotation(owner, weights)
    outgoing = outgoing.reshape(SHARDS * EIGHT, EIGHT * GROUP, BLOCK)
    received = lax.all_to_all(outgoing, ("fsdp", "tp"), 0, 0, tiled=True)
    received = received.reshape(SHARDS * EIGHT, EIGHT, GROUP, BLOCK)
    received, meta = lax.optimization_barrier((received, meta))
    return lax.cond(meta[META_FITS, 0] != 0, packed, general, meta, received)


def solution(mesh):
    return jax.shard_map(
        per_device,
        mesh=mesh,
        in_specs=(P("fsdp", "tp"), P()),
        out_specs=(P("fsdp", "tp"), P("fsdp", "tp")),
        check_vma=False,
    )
```

```python
import functools

import jax
import jax.numpy as jnp
from jax import lax
from jax.experimental import pallas as pl
from jax.experimental.pallas import tpu as pltpu
from jax.sharding import PartitionSpec as P

BLOCK = 128
LANES = 128
GROUP = 16
EIGHT = 8
SHARDS = 16
TILES = 8
PAIRS = 4
STEP_SLOTS = 4
SIDE = 4
PACKED = 12
META_RANK, META_POS, META_SLOT, META_HOT, META_FITS, META_OWNER = range(6)
F32 = jnp.float32
BF16 = jnp.bfloat16


def butterflies(values):
    values = list(values)
    span = 1
    while span < len(values):
        for base in range(0, len(values), 2 * span):
            for k in range(base, base + span):
                low, high = values[k], values[k + span]
                values[k], values[k + span] = low + high, low - high
        span *= 2
    return values


def parity_signs(bits, scale):
    shift = 4
    while shift:
        bits = bits ^ (bits >> shift)
        shift //= 2
    return jnp.where((bits & 1) == 0, scale, -scale).astype(BF16)


def identity(size):
    row = lax.broadcasted_iota(jnp.int32, (size, size), 0)
    col = lax.broadcasted_iota(jnp.int32, (size, size), 1)
    return jnp.where(row == col, 1.0, 0.0).astype(BF16)


def transposed(eye, value):
    return lax.dot_general(
        eye, value, (((1,), (1,)), ((), ())), preferred_element_type=F32
    ).astype(BF16)


def fill_tables(owner_row, me, meta_ref):
    shape = (BLOCK, BLOCK)
    by_lane = jnp.broadcast_to(owner_row.astype(F32), shape)
    by_row = by_lane.T
    row = lax.broadcasted_iota(jnp.int32, shape, 0)
    lane = lax.broadcasted_iota(jnp.int32, shape, 1)
    equal = by_lane == by_row

    def count(mask, axis):
        total = jnp.sum(jnp.where(mask, 1.0, 0.0), axis=axis, keepdims=True)
        return total.astype(jnp.int32)

    total = count(equal, 0)
    position = count(equal & (row < lane), 0)
    position_by_row = count(equal & (lane < row), 1)
    hot = jnp.max(jnp.where(total == SHARDS, owner_row, -1), axis=1, keepdims=True)
    x, z = hot >> 2, hot & (SIDE - 1)
    around = [
        (((x + 1) & (SIDE - 1)) << 2) | z,
        (((x - 1) & (SIDE - 1)) << 2) | z,
        (x << 2) | ((z + 1) & (SIDE - 1)),
        (x << 2) | ((z - 1) & (SIDE - 1)),
    ]
    is_hot = owner_row == hot
    is_near = functools.reduce(jnp.logical_or, [owner_row == near for near in around])
    load = jnp.where(is_hot, 0, total + is_near.astype(jnp.int32))
    fits = (jnp.max(load, axis=1, keepdims=True) <= PACKED) & (hot >= 0)
    fits = jnp.broadcast_to(fits.astype(jnp.int32), owner_row.shape) != 0
    over = is_hot & (position >= PACKED) & fits
    rank = owner_row
    for d, near in enumerate(around):
        rank = jnp.where(over & (position == PACKED + d), near, rank)
    block = lane[:1]
    position = jnp.where(fits, jnp.where(over, PACKED - 1, position), block >> 3)
    mine = (by_row == me.astype(F32)) & ((row >> 3) == lane)
    slot = jnp.sum(
        jnp.where(mine, (position_by_row + 1).astype(F32), 0.0), axis=0, keepdims=True
    ).astype(jnp.int32) - 1
    slot = jnp.where(fits | (slot < 0), slot, block)
    meta_ref[META_RANK : META_RANK + 1, :] = rank
    meta_ref[META_POS : META_POS + 1, :] = position
    meta_ref[META_SLOT : META_SLOT + 1, :] = slot
    meta_ref[META_HOT : META_HOT + 1, :] = jnp.broadcast_to(hot, owner_row.shape)
    meta_ref[META_FITS : META_FITS + 1, :] = fits.astype(jnp.int32)
    meta_ref[META_OWNER : META_OWNER + 1, :] = owner_row


def local_kernel(owner_ref, w_ref, out_ref, meta_ref, sign_ref, eye_ref):
    @pl.when(pl.program_id(0) == 0)
    def _():
        row = lax.broadcasted_iota(jnp.int32, (256, 256), 0)
        col = lax.broadcasted_iota(jnp.int32, (256, 256), 1)
        sign_ref[...] = parity_signs(row & col, 1.0 / 32.0)
        eye_ref[...] = identity(256)
        fill_tables(owner_ref[...], lax.axis_index("fsdp"), meta_ref)

    for pair in range(TILES // 2):
        lanes = slice(2 * pair * LANES, 2 * (pair + 1) * LANES)
        mixed = butterflies([w_ref[256 * q : 256 * (q + 1), lanes] for q in range(4)])
        for q in range(4):
            turned = transposed(eye_ref[...], mixed[q].astype(BF16))
            half = jnp.dot(turned, sign_ref[...], preferred_element_type=F32).astype(BF16)
            for tile in range(2):
                for g in range(EIGHT):
                    row = (tile * EIGHT + g) * GROUP
                    for side in range(2):
                        out_ref[0, g, 2 * pair + tile, 2 * q + side] = half[
                            row : row + GROUP, side * BLOCK : (side + 1) * BLOCK
                        ]


def local_rotation(owner, weights):
    rows, cols = weights.shape
    steps = cols // (TILES * LANES)
    per_half = steps // 2
    return pl.pallas_call(
        local_kernel,
        grid=(steps,),
        in_specs=[
            pl.BlockSpec((1, BLOCK), lambda s: (0, 0)),
            pl.BlockSpec((rows, TILES * LANES), lambda s: (0, s)),
        ],
        out_specs=[
            pl.BlockSpec(
                (1, EIGHT, TILES, EIGHT, GROUP, BLOCK),
                lambda s: (s // per_half, 0, s % per_half, 0, 0, 0),
            ),
            pl.BlockSpec((EIGHT, BLOCK), lambda s: (0, 0)),
        ],
        out_shape=[
            jax.ShapeDtypeStruct((2, EIGHT, EIGHT, EIGHT, GROUP, BLOCK), BF16),
            jax.ShapeDtypeStruct((EIGHT, BLOCK), jnp.int32),
        ],
        scratch_shapes=[pltpu.VMEM((256, 256), BF16), pltpu.VMEM((256, 256), BF16)],
        name="local_rotation",
    )(owner.reshape(1, BLOCK), weights)


def quantize_kernel(
    meta_ref, in_ref, out_ref,
    received, held, sign_ref, block_scales, slot_scales, tail,
    in_sems, out_sem, tail_sem,
):
    def fetch(pair):
        return pltpu.make_async_copy(
            in_ref.at[:, pl.ds(2 * pair, 2)], received.at[pair], in_sems.at[pair]
        )

    for pair in range(PAIRS):
        fetch(pair).start()

    slot_scales[...] = jnp.zeros_like(slot_scales)
    row = lax.broadcasted_iota(jnp.int32, (256, 256), 0)
    col = lax.broadcasted_iota(jnp.int32, (256, 256), 1)
    signs = parity_signs((row // GROUP) & (col // GROUP), 0.25)
    same = (row & (GROUP - 1)) == (col & (GROUP - 1))
    sign_ref[...] = jnp.where(same, signs.astype(F32), 0.0).astype(BF16)

    @pl.loop(0, PAIRS)
    def _(pair):
        fetch(pair).wait()
        lane = lax.broadcasted_iota(jnp.int32, (SHARDS * GROUP, LANES), 1)
        for t in range(EIGHT):
            stacked = jnp.concatenate(
                [
                    jnp.concatenate(
                        [received[pair, a * EIGHT + t, side] for a in range(SHARDS)], axis=0
                    )
                    for side in range(2)
                ],
                axis=1,
            )
            mixed = jnp.dot(sign_ref[...], stacked, preferred_element_type=F32)
            for side in range(2):
                value = mixed[:, side * BLOCK : (side + 1) * BLOCK]
                largest = jnp.max(jnp.abs(value), axis=1, keepdims=True)
                scale = (largest + 1e-06).astype(BF16).astype(F32)
                ratio = (value * (1.0 / scale)).astype(BF16)
                pltpu.store(
                    block_scales.at[side],
                    jnp.broadcast_to(scale, lane.shape),
                    mask=lane // GROUP == t,
                )
                for a in range(SHARDS):
                    held[2 * pair + side, a, t * GROUP : (t + 1) * GROUP, :] = ratio[
                        a * GROUP : (a + 1) * GROUP
                    ]
        slot_lane = lane[:GROUP] & (GROUP - 1)
        for side in range(2):
            for a in range(SHARDS):
                block = a * EIGHT + 2 * pair + side
                start = pl.multiple_of(meta_ref[META_POS, block] * BLOCK, BLOCK)
                pltpu.make_async_copy(
                    held.at[2 * pair + side, a],
                    out_ref.at[meta_ref[META_RANK, block], pl.ds(start, BLOCK)],
                    out_sem,
                ).start()
                pltpu.store(
                    slot_scales.at[meta_ref[META_OWNER, block]],
                    block_scales[side, a * GROUP : (a + 1) * GROUP, :],
                    mask=slot_lane == a,
                )

    tail[...] = slot_scales[...].astype(BF16)
    tail_copy = pltpu.make_async_copy(
        tail, out_ref.at[:, pl.ds(out_ref.shape[1] - GROUP, GROUP), :], tail_sem
    )
    tail_copy.start()
    pltpu.make_async_copy(held, held, out_sem).wait()
    tail_copy.wait()


def quantize_blocks(meta, received, capacity):
    out_rows = capacity * BLOCK + GROUP
    sources = received.shape[0]
    return pl.pallas_call(
        quantize_kernel,
        in_specs=[
            pl.BlockSpec(memory_space=pltpu.SMEM),
            pl.BlockSpec(memory_space=pl.ANY),
        ],
        out_specs=pl.BlockSpec(memory_space=pl.ANY),
        scratch_shapes=[
            pltpu.VMEM((PAIRS, sources, 2, GROUP, BLOCK), BF16),
            pltpu.VMEM((EIGHT, SHARDS, BLOCK, BLOCK), BF16),
            pltpu.VMEM((256, 256), BF16),
            pltpu.VMEM((2, SHARDS * GROUP, LANES), F32),
            pltpu.VMEM((SHARDS, GROUP, LANES), F32),
            pltpu.VMEM((SHARDS, GROUP, LANES), BF16),
            pltpu.SemaphoreType.DMA((PAIRS,)),
            pltpu.SemaphoreType.DMA,
            pltpu.SemaphoreType.DMA,
        ],
        out_shape=jax.ShapeDtypeStruct((SHARDS, out_rows, LANES), BF16),
        name="quantize_blocks",
    )(meta, received)


def place_block(eye, source, target):
    for t in range(EIGHT):
        stacked = jnp.concatenate(
            [source[m, t * GROUP : (t + 1) * GROUP, :] for m in range(SHARDS)], axis=0
        )
        target[:, t * 2 * LANES : (t + 1) * 2 * LANES] = transposed(eye, stacked)


def place_kernel(capacity, meta_ref, *refs):
    ins, (scale_in_ref, out_ref, scale_out_ref, eye_ref) = refs[:STEP_SLOTS], refs[STEP_SLOTS:]

    @pl.when(pl.program_id(0) == 0)
    def _():
        eye_ref[...] = identity(BLOCK)
        stacked = jnp.concatenate([scale_in_ref[m] for m in range(SHARDS)], axis=0)
        by_column = transposed(eye_ref[...], stacked)
        for t in range(EIGHT):
            scale_out_ref[:, t * 2 * LANES : (t + 1) * 2 * LANES] = by_column[
                t * GROUP : (t + 1) * GROUP
            ]

    for k in range(STEP_SLOTS):
        target = out_ref.at[pl.ds(k * BLOCK, BLOCK), :]
        source = meta_ref[META_SLOT, pl.program_id(0) * STEP_SLOTS + k]
        taken = (source >= 0) & (source < capacity)

        @pl.when(taken)
        def _():
            place_block(eye_ref[...], ins[k], target)

        @pl.when(jnp.logical_not(taken))
        def _():
            target[...] = jnp.zeros(target.shape, BF16)


def place_columns(meta, incoming, capacity):
    cols = SHARDS * LANES
    step_rows = STEP_SLOTS * BLOCK

    def slot_map(k):
        def index(s, meta_ref):
            source = meta_ref[META_SLOT, s * STEP_SLOTS + k]
            return (0, jnp.clip(source, 0, capacity - 1), 0)

        return index

    return pl.pallas_call(
        functools.partial(place_kernel, capacity),
        grid_spec=pltpu.PrefetchScalarGridSpec(
            num_scalar_prefetch=1,
            grid=(SHARDS // STEP_SLOTS,),
            in_specs=[
                pl.BlockSpec((SHARDS, BLOCK, LANES), slot_map(k)) for k in range(STEP_SLOTS)
            ]
            + [pl.BlockSpec((SHARDS, GROUP, LANES), lambda s, _: (0, capacity * EIGHT, 0))],
            out_specs=[
                pl.BlockSpec((step_rows, cols), lambda s, _: (s, 0)),
                pl.BlockSpec((SHARDS, cols), lambda s, _: (0, 0)),
            ],
            scratch_shapes=[pltpu.VMEM((BLOCK, BLOCK), BF16)],
        ),
        out_shape=[
            jax.ShapeDtypeStruct((SHARDS * BLOCK, cols), BF16),
            jax.ShapeDtypeStruct((SHARDS, cols), BF16),
        ],
        cost_estimate=pl.CostEstimate(
            flops=2 * SHARDS * BLOCK * BLOCK * cols,
            bytes_accessed=4 * SHARDS * BLOCK * cols,
            transcendentals=0,
        ),
        compiler_params=pltpu.CompilerParams(vmem_limit_bytes=46 << 20),
        name="place_columns",
    )(meta, *[incoming] * (STEP_SLOTS + 1))


def copy_kernel(in_ref, out_ref):
    out_ref[...] = in_ref[...]


def last_position(incoming):
    shape = (SHARDS, BLOCK, LANES)
    return pl.pallas_call(
        copy_kernel,
        grid=(1,),
        in_specs=[pl.BlockSpec(shape, lambda s: (0, PACKED - 1, 0))],
        out_specs=pl.BlockSpec(shape, lambda s: (0, 0, 0)),
        out_shape=jax.ShapeDtypeStruct(shape, BF16),
        compiler_params=pltpu.CompilerParams(vmem_limit_bytes=4 << 20),
        name="last_position",
    )(incoming)


def patch_kernel(
    meta_ref, near_0, near_1, near_2, near_3, _, out_ref, nears, buffers, eye_ref, in_sem, sem
):
    @pl.when(meta_ref[META_HOT, 0] == lax.axis_index("fsdp"))
    def _():
        loads = [
            pltpu.make_async_copy(near, nears.at[d], in_sem.at[d])
            for d, near in enumerate((near_0, near_1, near_2, near_3))
        ]
        for load in loads:
            load.start()
        eye_ref[...] = identity(BLOCK)
        stores = []
        for d, load in enumerate(loads):
            load.wait()
            place_block(eye_ref[...], nears.at[d], buffers.at[d])
            stores.append(
                pltpu.make_async_copy(
                    buffers.at[d], out_ref.at[pl.ds((PACKED + d) * BLOCK, BLOCK), :], sem.at[d]
                )
            )
            stores[-1].start()
        for store in stores:
            store.wait()


def patch_hot_rank(meta, rolled, nears):
    cols = rolled.shape[1]
    return pl.pallas_call(
        patch_kernel,
        in_specs=[pl.BlockSpec(memory_space=pltpu.SMEM)]
        + [pl.BlockSpec(memory_space=pl.ANY)] * 5,
        out_specs=pl.BlockSpec(memory_space=pl.ANY),
        out_shape=jax.ShapeDtypeStruct(rolled.shape, rolled.dtype),
        scratch_shapes=[
            pltpu.VMEM((4, SHARDS, BLOCK, LANES), BF16),
            pltpu.VMEM((4, BLOCK, cols), BF16),
            pltpu.VMEM((BLOCK, BLOCK), BF16),
            pltpu.SemaphoreType.DMA((4,)),
            pltpu.SemaphoreType.DMA((4,)),
        ],
        input_output_aliases={5: 0},
        compiler_params=pltpu.CompilerParams(vmem_limit_bytes=50 << 20),
        name="patch_hot_rank",
    )(meta, *nears, rolled)


def shifted(value, dx, dz):
    pairs = []
    for source in range(SHARDS):
        x, z = divmod(source, SIDE)
        pairs.append((source, (x + dx) % SIDE * SIDE + (z + dz) % SIDE))
    return lax.ppermute(value, "fsdp", pairs)


def general(meta, received):
    slotted = quantize_blocks(meta, received, SHARDS)
    incoming = lax.all_to_all(slotted, "fsdp", 0, 0, tiled=True)
    return tuple(place_columns(meta, incoming, SHARDS))


def packed(meta, received):
    slotted = quantize_blocks(meta, received, PACKED)
    incoming = lax.all_to_all(slotted, "fsdp", 0, 0, tiled=True)
    foreign = last_position(incoming)
    nears = [shifted(foreign, dx, dz) for dx, dz in ((-1, 0), (1, 0), (0, -1), (0, 1))]
    rolled, rolled_scales = place_columns(meta, incoming, PACKED)
    return patch_hot_rank(meta, rolled, nears), rolled_scales


def per_device(weights, owner):
    outgoing, meta = local_rotation(owner, weights)
    outgoing = outgoing.reshape(SHARDS * EIGHT, EIGHT * GROUP, BLOCK)
    received = lax.all_to_all(outgoing, ("fsdp", "tp"), 0, 0, tiled=True)
    received = received.reshape(SHARDS * EIGHT, EIGHT, GROUP, BLOCK)
    received, meta = lax.optimization_barrier((received, meta))
    return lax.cond(meta[META_FITS, 0] != 0, packed, general, meta, received)


def solution(mesh):
    return jax.shard_map(
        per_device,
        mesh=mesh,
        in_specs=(P("fsdp", "tp"), P()),
        out_specs=(P("fsdp", "tp"), P("fsdp", "tp")),
        check_vma=False,
    )
```

```python
import functools

import jax
import jax.numpy as jnp
from jax import lax
from jax.experimental import pallas as pl
from jax.experimental.pallas import tpu as pltpu
from jax.sharding import PartitionSpec as P

BLOCK = 128
LANES = 128
GROUP = 16
EIGHT = 8
SHARDS = 16
TILES = 8
PAIRS = 4
STEP_SLOTS = 4
SIDE = 4
CAPACITIES = (16, 13, 12)
META_RANK, META_POS, META_SLOT, META_HOT, META_LEVEL, META_OWNER = range(6)
F32 = jnp.float32
BF16 = jnp.bfloat16


def butterflies(values):
    values = list(values)
    span = 1
    while span < len(values):
        for base in range(0, len(values), 2 * span):
            for k in range(base, base + span):
                low, high = values[k], values[k + span]
                values[k], values[k + span] = low + high, low - high
        span *= 2
    return values


def parity_signs(bits, scale):
    shift = 4
    while shift:
        bits = bits ^ (bits >> shift)
        shift //= 2
    return jnp.where((bits & 1) == 0, scale, -scale).astype(BF16)


def identity(size):
    row = lax.broadcasted_iota(jnp.int32, (size, size), 0)
    col = lax.broadcasted_iota(jnp.int32, (size, size), 1)
    return jnp.where(row == col, 1.0, 0.0).astype(BF16)


def transposed(eye, value):
    return lax.dot_general(
        eye, value, (((1,), (1,)), ((), ())), preferred_element_type=F32
    ).astype(BF16)


def fill_tables(owner_row, me, meta_ref):
    shape = (BLOCK, BLOCK)
    by_lane = jnp.broadcast_to(owner_row.astype(F32), shape)
    by_row = by_lane.T
    row = lax.broadcasted_iota(jnp.int32, shape, 0)
    lane = lax.broadcasted_iota(jnp.int32, shape, 1)
    equal = by_lane == by_row

    def count(mask, axis):
        total = jnp.sum(jnp.where(mask, 1.0, 0.0), axis=axis, keepdims=True)
        return total.astype(jnp.int32)

    total = count(equal, 0)
    position = count(equal & (row < lane), 0)
    position_by_row = count(equal & (lane < row), 1)
    hot = jnp.max(jnp.where(total == SHARDS, owner_row, -1), axis=1, keepdims=True)
    x, z = hot >> 2, hot & (SIDE - 1)
    around = [
        (((x + 1) & (SIDE - 1)) << 2) | z,
        (((x - 1) & (SIDE - 1)) << 2) | z,
        (x << 2) | ((z + 1) & (SIDE - 1)),
        (x << 2) | ((z - 1) & (SIDE - 1)),
    ]
    is_hot = owner_row == hot
    level = jnp.zeros_like(hot)
    capacity = jnp.full_like(hot, SHARDS)
    for choice in (1, 2):
        size = CAPACITIES[choice]
        is_near = functools.reduce(
            jnp.logical_or, [owner_row == near for near in around[: SHARDS - size]]
        )
        load = jnp.where(is_hot, 0, total + is_near.astype(jnp.int32))
        good = (jnp.max(load, axis=1, keepdims=True) <= size) & (hot >= 0)
        level = jnp.where(good, choice, level)
        capacity = jnp.where(good, size, capacity)
    level = jnp.broadcast_to(level, owner_row.shape)
    capacity = jnp.broadcast_to(capacity, owner_row.shape)
    fits = level > 0
    over = is_hot & (position >= capacity) & fits
    rank = owner_row
    for d, near in enumerate(around):
        rank = jnp.where(over & (position == capacity + d), near, rank)
    block = lane[:1]
    position = jnp.where(fits, jnp.where(over, capacity - 1, position), block >> 3)
    mine = (by_row == me.astype(F32)) & ((row >> 3) == lane)
    slot = jnp.sum(
        jnp.where(mine, (position_by_row + 1).astype(F32), 0.0), axis=0, keepdims=True
    ).astype(jnp.int32) - 1
    slot = jnp.where(fits | (slot < 0), slot, block)
    meta_ref[META_RANK : META_RANK + 1, :] = rank
    meta_ref[META_POS : META_POS + 1, :] = position
    meta_ref[META_SLOT : META_SLOT + 1, :] = slot
    meta_ref[META_HOT : META_HOT + 1, :] = jnp.broadcast_to(hot, owner_row.shape)
    meta_ref[META_LEVEL : META_LEVEL + 1, :] = level
    meta_ref[META_OWNER : META_OWNER + 1, :] = owner_row


def local_kernel(owner_ref, w_ref, out_ref, meta_ref, sign_ref, eye_ref):
    @pl.when(pl.program_id(0) == 0)
    def _():
        row = lax.broadcasted_iota(jnp.int32, (256, 256), 0)
        col = lax.broadcasted_iota(jnp.int32, (256, 256), 1)
        sign_ref[...] = parity_signs(row & col, 1.0 / 32.0)
        eye_ref[...] = identity(256)
        fill_tables(owner_ref[...], lax.axis_index("fsdp"), meta_ref)

    for pair in range(TILES // 2):
        lanes = slice(2 * pair * LANES, 2 * (pair + 1) * LANES)
        mixed = butterflies([w_ref[256 * q : 256 * (q + 1), lanes] for q in range(4)])
        for q in range(4):
            turned = transposed(eye_ref[...], mixed[q].astype(BF16))
            half = jnp.dot(turned, sign_ref[...], preferred_element_type=F32).astype(BF16)
            for tile in range(2):
                for g in range(EIGHT):
                    row = (tile * EIGHT + g) * GROUP
                    for side in range(2):
                        out_ref[0, g, 2 * pair + tile, 2 * q + side] = half[
                            row : row + GROUP, side * BLOCK : (side + 1) * BLOCK
                        ]


def local_rotation(owner, weights):
    rows, cols = weights.shape
    steps = cols // (TILES * LANES)
    per_half = steps // 2
    return pl.pallas_call(
        local_kernel,
        grid=(steps,),
        in_specs=[
            pl.BlockSpec((1, BLOCK), lambda s: (0, 0)),
            pl.BlockSpec((rows, TILES * LANES), lambda s: (0, s)),
        ],
        out_specs=[
            pl.BlockSpec(
                (1, EIGHT, TILES, EIGHT, GROUP, BLOCK),
                lambda s: (s // per_half, 0, s % per_half, 0, 0, 0),
            ),
            pl.BlockSpec((EIGHT, BLOCK), lambda s: (0, 0)),
        ],
        out_shape=[
            jax.ShapeDtypeStruct((2, EIGHT, EIGHT, EIGHT, GROUP, BLOCK), BF16),
            jax.ShapeDtypeStruct((EIGHT, BLOCK), jnp.int32),
        ],
        scratch_shapes=[pltpu.VMEM((256, 256), BF16), pltpu.VMEM((256, 256), BF16)],
        name="local_rotation",
    )(owner.reshape(1, BLOCK), weights)


def quantize_kernel(
    meta_ref, in_ref, out_ref,
    received, held, sign_ref, block_scales, slot_scales, tail,
    in_sems, out_sem, tail_sem,
):
    def fetch(pair):
        return pltpu.make_async_copy(
            in_ref.at[:, pl.ds(2 * pair, 2)], received.at[pair], in_sems.at[pair]
        )

    for pair in range(PAIRS):
        fetch(pair).start()

    slot_scales[...] = jnp.zeros_like(slot_scales)
    row = lax.broadcasted_iota(jnp.int32, (256, 256), 0)
    col = lax.broadcasted_iota(jnp.int32, (256, 256), 1)
    signs = parity_signs((row // GROUP) & (col // GROUP), 0.25)
    same = (row & (GROUP - 1)) == (col & (GROUP - 1))
    sign_ref[...] = jnp.where(same, signs.astype(F32), 0.0).astype(BF16)

    @pl.loop(0, PAIRS)
    def _(pair):
        fetch(pair).wait()
        lane = lax.broadcasted_iota(jnp.int32, (SHARDS * GROUP, LANES), 1)
        for t in range(EIGHT):
            stacked = jnp.concatenate(
                [
                    jnp.concatenate(
                        [received[pair, a * EIGHT + t, side] for a in range(SHARDS)], axis=0
                    )
                    for side in range(2)
                ],
                axis=1,
            )
            mixed = jnp.dot(sign_ref[...], stacked, preferred_element_type=F32)
            for side in range(2):
                value = mixed[:, side * BLOCK : (side + 1) * BLOCK]
                largest = jnp.max(jnp.abs(value), axis=1, keepdims=True)
                scale = (largest + 1e-06).astype(BF16).astype(F32)
                ratio = (value * (1.0 / scale)).astype(BF16)
                pltpu.store(
                    block_scales.at[side],
                    jnp.broadcast_to(scale, lane.shape),
                    mask=lane // GROUP == t,
                )
                for a in range(SHARDS):
                    held[2 * pair + side, a, t * GROUP : (t + 1) * GROUP, :] = ratio[
                        a * GROUP : (a + 1) * GROUP
                    ]
        slot_lane = lane[:GROUP] & (GROUP - 1)
        for side in range(2):
            for a in range(SHARDS):
                block = a * EIGHT + 2 * pair + side
                start = pl.multiple_of(meta_ref[META_POS, block] * BLOCK, BLOCK)
                pltpu.make_async_copy(
                    held.at[2 * pair + side, a],
                    out_ref.at[meta_ref[META_RANK, block], pl.ds(start, BLOCK)],
                    out_sem,
                ).start()
                pltpu.store(
                    slot_scales.at[meta_ref[META_OWNER, block]],
                    block_scales[side, a * GROUP : (a + 1) * GROUP, :],
                    mask=slot_lane == a,
                )

    tail[...] = slot_scales[...].astype(BF16)
    tail_copy = pltpu.make_async_copy(
        tail, out_ref.at[:, pl.ds(out_ref.shape[1] - GROUP, GROUP), :], tail_sem
    )
    tail_copy.start()
    pltpu.make_async_copy(held, held, out_sem).wait()
    tail_copy.wait()


def quantize_blocks(meta, received, capacity):
    out_rows = capacity * BLOCK + GROUP
    sources = received.shape[0]
    return pl.pallas_call(
        quantize_kernel,
        in_specs=[
            pl.BlockSpec(memory_space=pltpu.SMEM),
            pl.BlockSpec(memory_space=pl.ANY),
        ],
        out_specs=pl.BlockSpec(memory_space=pl.ANY),
        scratch_shapes=[
            pltpu.VMEM((PAIRS, sources, 2, GROUP, BLOCK), BF16),
            pltpu.VMEM((EIGHT, SHARDS, BLOCK, BLOCK), BF16),
            pltpu.VMEM((256, 256), BF16),
            pltpu.VMEM((2, SHARDS * GROUP, LANES), F32),
            pltpu.VMEM((SHARDS, GROUP, LANES), F32),
            pltpu.VMEM((SHARDS, GROUP, LANES), BF16),
            pltpu.SemaphoreType.DMA((PAIRS,)),
            pltpu.SemaphoreType.DMA,
            pltpu.SemaphoreType.DMA,
        ],
        out_shape=jax.ShapeDtypeStruct((SHARDS, out_rows, LANES), BF16),
        name="quantize_blocks",
    )(meta, received)


def place_block(eye, source, target):
    for t in range(EIGHT):
        stacked = jnp.concatenate(
            [source[m, t * GROUP : (t + 1) * GROUP, :] for m in range(SHARDS)], axis=0
        )
        target[:, t * 2 * LANES : (t + 1) * 2 * LANES] = transposed(eye, stacked)


def place_kernel(capacity, meta_ref, *refs):
    ins, (scale_in_ref, out_ref, scale_out_ref, eye_ref) = refs[:STEP_SLOTS], refs[STEP_SLOTS:]

    @pl.when(pl.program_id(0) == 0)
    def _():
        eye_ref[...] = identity(BLOCK)
        stacked = jnp.concatenate([scale_in_ref[m] for m in range(SHARDS)], axis=0)
        by_column = transposed(eye_ref[...], stacked)
        for t in range(EIGHT):
            scale_out_ref[:, t * 2 * LANES : (t + 1) * 2 * LANES] = by_column[
                t * GROUP : (t + 1) * GROUP
            ]

    for k in range(STEP_SLOTS):
        target = out_ref.at[pl.ds(k * BLOCK, BLOCK), :]
        source = meta_ref[META_SLOT, pl.program_id(0) * STEP_SLOTS + k]
        taken = (source >= 0) & (source < capacity)

        @pl.when(taken)
        def _():
            place_block(eye_ref[...], ins[k], target)

        @pl.when(jnp.logical_not(taken))
        def _():
            target[...] = jnp.zeros(target.shape, BF16)


def place_columns(meta, incoming, capacity):
    cols = SHARDS * LANES
    step_rows = STEP_SLOTS * BLOCK

    def slot_map(k):
        def index(s, meta_ref):
            source = meta_ref[META_SLOT, s * STEP_SLOTS + k]
            return (0, jnp.clip(source, 0, capacity - 1), 0)

        return index

    return pl.pallas_call(
        functools.partial(place_kernel, capacity),
        grid_spec=pltpu.PrefetchScalarGridSpec(
            num_scalar_prefetch=1,
            grid=(SHARDS // STEP_SLOTS,),
            in_specs=[
                pl.BlockSpec((SHARDS, BLOCK, LANES), slot_map(k)) for k in range(STEP_SLOTS)
            ]
            + [pl.BlockSpec((SHARDS, GROUP, LANES), lambda s, _: (0, capacity * EIGHT, 0))],
            out_specs=[
                pl.BlockSpec((step_rows, cols), lambda s, _: (s, 0)),
                pl.BlockSpec((SHARDS, cols), lambda s, _: (0, 0)),
            ],
            scratch_shapes=[pltpu.VMEM((BLOCK, BLOCK), BF16)],
        ),
        out_shape=[
            jax.ShapeDtypeStruct((SHARDS * BLOCK, cols), BF16),
            jax.ShapeDtypeStruct((SHARDS, cols), BF16),
        ],
        cost_estimate=pl.CostEstimate(
            flops=2 * SHARDS * BLOCK * BLOCK * cols,
            bytes_accessed=4 * SHARDS * BLOCK * cols,
            transcendentals=0,
        ),
        compiler_params=pltpu.CompilerParams(vmem_limit_bytes=46 << 20),
        name="place_columns",
    )(meta, *[incoming] * (STEP_SLOTS + 1))


def copy_kernel(in_ref, out_ref):
    out_ref[...] = in_ref[...]


def last_position(incoming, capacity):
    shape = (SHARDS, BLOCK, LANES)
    return pl.pallas_call(
        copy_kernel,
        grid=(1,),
        in_specs=[pl.BlockSpec(shape, lambda s: (0, capacity - 1, 0))],
        out_specs=pl.BlockSpec(shape, lambda s: (0, 0, 0)),
        out_shape=jax.ShapeDtypeStruct(shape, BF16),
        compiler_params=pltpu.CompilerParams(vmem_limit_bytes=4 << 20),
        name="last_position",
    )(incoming)


def patch_kernel(capacity, meta_ref, *refs):
    count = SHARDS - capacity
    arrived, (_, out_ref, nears, buffers, eye_ref, in_sem, sem) = refs[:count], refs[count:]

    @pl.when(meta_ref[META_HOT, 0] == lax.axis_index("fsdp"))
    def _():
        loads = [
            pltpu.make_async_copy(near, nears.at[d], in_sem.at[d])
            for d, near in enumerate(arrived)
        ]
        for load in loads:
            load.start()
        eye_ref[...] = identity(BLOCK)
        stores = []
        for d, load in enumerate(loads):
            load.wait()
            place_block(eye_ref[...], nears.at[d], buffers.at[d])
            stores.append(
                pltpu.make_async_copy(
                    buffers.at[d], out_ref.at[pl.ds((capacity + d) * BLOCK, BLOCK), :], sem.at[d]
                )
            )
            stores[-1].start()
        for store in stores:
            store.wait()


def patch_hot_rank(meta, rolled, nears):
    cols = rolled.shape[1]
    count = len(nears)
    return pl.pallas_call(
        functools.partial(patch_kernel, SHARDS - count),
        in_specs=[pl.BlockSpec(memory_space=pltpu.SMEM)]
        + [pl.BlockSpec(memory_space=pl.ANY)] * (count + 1),
        out_specs=pl.BlockSpec(memory_space=pl.ANY),
        out_shape=jax.ShapeDtypeStruct(rolled.shape, rolled.dtype),
        scratch_shapes=[
            pltpu.VMEM((count, SHARDS, BLOCK, LANES), BF16),
            pltpu.VMEM((count, BLOCK, cols), BF16),
            pltpu.VMEM((BLOCK, BLOCK), BF16),
            pltpu.SemaphoreType.DMA((count,)),
            pltpu.SemaphoreType.DMA((count,)),
        ],
        input_output_aliases={count + 1: 0},
        compiler_params=pltpu.CompilerParams(vmem_limit_bytes=50 << 20),
        name="patch_hot_rank",
    )(meta, *nears, rolled)


def shifted(value, dx, dz):
    pairs = []
    for source in range(SHARDS):
        x, z = divmod(source, SIDE)
        pairs.append((source, (x + dx) % SIDE * SIDE + (z + dz) % SIDE))
    return lax.ppermute(value, "fsdp", pairs)


def general(meta, received):
    slotted = quantize_blocks(meta, received, SHARDS)
    incoming = lax.all_to_all(slotted, "fsdp", 0, 0, tiled=True)
    return tuple(place_columns(meta, incoming, SHARDS))


def packed(capacity, meta, received):
    slotted = quantize_blocks(meta, received, capacity)
    incoming = lax.all_to_all(slotted, "fsdp", 0, 0, tiled=True)
    foreign = last_position(incoming, capacity)
    ways = ((-1, 0), (1, 0), (0, -1), (0, 1))[: SHARDS - capacity]
    nears = [shifted(foreign, dx, dz) for dx, dz in ways]
    rolled, rolled_scales = place_columns(meta, incoming, capacity)
    return patch_hot_rank(meta, rolled, nears), rolled_scales


def per_device(weights, owner):
    outgoing, meta = local_rotation(owner, weights)
    outgoing = outgoing.reshape(SHARDS * EIGHT, EIGHT * GROUP, BLOCK)
    received = lax.all_to_all(outgoing, ("fsdp", "tp"), 0, 0, tiled=True)
    received = received.reshape(SHARDS * EIGHT, EIGHT, GROUP, BLOCK)
    received, meta = lax.optimization_barrier((received, meta))
    return lax.switch(
        meta[META_LEVEL, 0],
        [general] + [functools.partial(packed, size) for size in CAPACITIES[1:]],
        meta,
        received,
    )


def solution(mesh):
    return jax.shard_map(
        per_device,
        mesh=mesh,
        in_specs=(P("fsdp", "tp"), P()),
        out_specs=(P("fsdp", "tp"), P("fsdp", "tp")),
        check_vma=False,
    )
```
